512 devices in a mesh: dp: 32 (over y, x, core), seq: 16 (over z).
Axes of the slice: x: 4, y: 4, z: 16, core: 2. Of those that a mesh axis runs over, the one named last changes fastest.
Arguments:
- loader_rows: bfloat16 [3, 32, 1280, 4096], P(None, 'dp', 'seq'), may hold values from -6 to 6
- cotangent: bfloat16 [32, 1280, 4096], P('dp', None, 'seq'), may hold values from -6 to 6
- gains: float32 [2, 32, 128], P(None, 'seq'), may hold values from 0.25 to 1.75
- block_rows: int32 [32, 16, 32], replicated, may hold values from 0 to 3, as said below
- block_clip: int32 [32, 32], replicated, may hold values from 0 to 3
Outputs:
- gradients: bfloat16 [3, 32, 1280, 4096], P(None, 'dp', 'seq')
- gain_grads: float32 [2, 32, 128], P(None, 'seq')
The draws below stay inside these ranges and needn't reach their ends.
Inputs may be any that keep to these rules, and one draw needn't show every extreme that they name: `block_rows`: in every sequence shard, each loader shard sends at most 80 rows in all and each pack receives at most 80 rows in all; some loader shard sends and some pack receives exactly 80, and some block has exactly 3 rows.
All inputs are finite; a program needn't handle non-finite values.
Results may differ from the reference program's by a relative error of at most 0.0071.
Values may be sent and summed in bfloat16 or wider, within the bound.
No kernel may reach another device: no remote copies, remote signals or barrier semaphores. Data moves between devices by JAX's collectives and lax.ppermute only.
A program may use at most 64 MiB of HBM per device.

```python
import math
import jax
import jax.numpy as jnp
from jax import lax

HD = 128
CLIPS = 4
CAP = 80
HEADS = 32
PACK = 1280
SLOT = 3
N_DP = 32
N_SEQ = 16


def draw_block_rows(key, part):
    column_keys = jax.random.split(key, N_SEQ)

    def one_column(column_key):
        key_order, key_level, key_coin, key_pack, key_loader = jax.random.split(column_key, 5)
        base = CAP // N_DP
        extra = CAP % N_DP
        order = jax.random.permutation(key_order, N_DP)
        multiple = base + (order < extra).astype(jnp.int32)
        pack_ids = jnp.arange(N_DP, dtype=jnp.int32)[:, None]
        loader_ids = jnp.arange(N_DP, dtype=jnp.int32)[None, :]
        units = multiple[(pack_ids - loader_ids) % N_DP]
        levels = jax.random.randint(key_level, (N_DP, 1, 1), 4, 11)
        coins = jax.random.randint(key_coin, (N_DP, N_DP, SLOT), 0, 10)
        full_pack = jax.random.randint(key_pack, (), 0, N_DP)
        full_loader = jax.random.randint(key_loader, (), 0, N_DP)
        forced = (pack_ids == full_pack) | (loader_ids == full_loader)
        slot_ids = jnp.arange(SLOT, dtype=jnp.int32)
        live = (slot_ids[None, None, :] < units[:, :, None]) & ((coins < levels) | forced[:, :, None])
        return jnp.sum(live.astype(jnp.int32), axis=-1).astype(jnp.int32)
    table = jax.vmap(one_column)(column_keys)
    return jnp.transpose(table, (1, 0, 2))


def place_ends(values, rng, smallest, high):
    dims = values.shape
    spot = [jax.random.randint(jax.random.fold_in(rng, axis), (), 0, dims[axis]) for axis in range(len(dims))]
    values = values.at[tuple(spot)].set(smallest)
    longest = dims.index(max(dims))
    spot[longest] = (spot[longest] + 1) % dims[longest]
    return values.at[tuple(spot)].set(high)


def level_of(own_key, extent, cuts, least, top_value):
    def one(axis_at, shards_of):
        heights = jax.random.uniform(jax.random.fold_in(jax.random.fold_in(own_key, 6), axis_at), (shards_of,), jnp.float32, least / len(cuts), top_value / len(cuts))
        return jnp.repeat(jnp.exp(heights), extent[axis_at] // shards_of).reshape((-1,) + (1,) * (len(extent) - axis_at - 1))

    level = one(*cuts[0])
    for cut in cuts[1:]:
        level = level * one(*cut)
    return level


def gaussian(own_key, shape, width, most, shards=(), held_as=jnp.bfloat16):
    result = width * jax.random.normal(own_key, shape, jnp.float32)
    if shards:
        result = result * level_of(own_key, shape, shards, -0.22, 0.18)
    return jnp.clip(result, -most, most).astype(held_as)


def setup_inputs(seed: int = 0) -> dict:
    splits = jax.random.split(jax.random.key(seed), 6)
    loader_rows = gaussian(splits[0], (3, N_DP, PACK, HEADS * HD), 1.0, 6.0, ((1, 32), (2, 16)))
    cotangent = gaussian(splits[1], (N_DP, PACK, HEADS * HD), 1.0, 6.0, ((0, 32), (2, 16)))
    gains = jnp.clip(1.0 + 0.15 * jax.random.normal(splits[2], (2, HEADS, HD), jnp.float32), 0.25, 1.75)
    block_rows = draw_block_rows(jax.random.fold_in(splits[5], 71), 0)
    block_clip = place_ends(jax.random.randint(splits[4], (N_DP, N_DP), 0, CLIPS), jax.random.fold_in(splits[4], 1), 0, CLIPS - 1).astype(jnp.int32)
    return dict(loader_rows=loader_rows, cotangent=cotangent, gains=gains, block_rows=block_rows, block_clip=block_clip)


epsilon = 1e-06

def standardize(rows):
    centred = rows - lax.optimization_barrier(jnp.mean(rows, axis=-1, keepdims=True))
    spread = lax.optimization_barrier(jnp.mean(centred * centred, axis=-1, keepdims=True))
    factor = lax.rsqrt(spread + epsilon)
    return (centred * factor, factor)

def back_norm(grad_hat, normed, factor):
    first = lax.optimization_barrier(jnp.mean(grad_hat, axis=-1, keepdims=True))
    second = lax.optimization_barrier(jnp.mean(grad_hat * normed, axis=-1, keepdims=True))
    return factor * (grad_hat - first - normed * second)

def weighted_value_sum(form, left, right):
    return jnp.einsum(form, left.astype(jnp.float32), right.astype(jnp.float32), precision=lax.Precision.HIGHEST)

def head_grads(queries, key_rows, value_rows, cot_rows, labels, valid_rows, gain_query, gain_key):
    score_scale = 1.0 / math.sqrt(queries.shape[-1])
    query_hat, query_factor = standardize(queries.astype(jnp.float32))
    key_hat, key_factor = standardize(key_rows.astype(jnp.float32))
    query_norm_inverse = (query_hat * gain_query).astype(jnp.bfloat16)
    key_norm_inverse = (key_hat * gain_key).astype(jnp.bfloat16)
    logit_score = weighted_value_sum('nlf,nhf->nlh', query_norm_inverse, key_norm_inverse) * score_scale
    same_clip = labels[..., :, None] == labels[..., None, :]
    raw_weight = jnp.where(same_clip, jnp.exp(logit_score), 0.0)
    attention = raw_weight / lax.optimization_barrier(jnp.sum(raw_weight, axis=-1, keepdims=True))
    attention_weights_cast = attention.astype(jnp.bfloat16)
    attended_output = weighted_value_sum('mye,meo->myo', attention_weights_cast, value_rows)
    output_gradient = jnp.where(valid_rows[..., None], cot_rows, jnp.zeros((), cot_rows.dtype))
    value_gradient = weighted_value_sum('owh,owv->ohv', attention_weights_cast, output_gradient)
    attention_gradient = weighted_value_sum('nlf,nhf->nlh', output_gradient, value_rows)
    row_delta = lax.optimization_barrier(jnp.sum(output_gradient.astype(jnp.float32) * attended_output, axis=-1, keepdims=True))
    score_gradient = (attention * (attention_gradient - row_delta) * score_scale).astype(jnp.bfloat16)
    query_gradient = weighted_value_sum('mye,meo->myo', score_gradient, key_norm_inverse)
    key_gradient = weighted_value_sum('owh,owv->ohv', score_gradient, query_norm_inverse)
    grad_gq = lax.optimization_barrier(jnp.sum(query_gradient * query_hat, axis=1))
    grad_gk = lax.optimization_barrier(jnp.sum(key_gradient * key_hat, axis=1))
    grad_q = back_norm(query_gradient * gain_query, query_hat, query_factor).astype(jnp.bfloat16)
    grad_k = back_norm(key_gradient * gain_key, key_hat, key_factor).astype(jnp.bfloat16)
    return (grad_q, grad_k, value_gradient.astype(jnp.bfloat16), grad_gq, grad_gk)

def locate(counts, capacity):
    peers = counts.shape[-1]
    end_rows = jnp.cumsum(counts, axis=-1).astype(jnp.int32)
    start_rows = (end_rows - counts).astype(jnp.int32)
    places = jnp.arange(capacity, dtype=jnp.int32)
    source = lax.optimization_barrier(jnp.sum((end_rows[..., None, :] <= places[:, None]).astype(jnp.int32), axis=-1)).astype(jnp.int32)
    source = jnp.minimum(source, peers - 1)
    matches = source[..., None] == jnp.arange(peers, dtype=jnp.int32)
    begin_at = lax.optimization_barrier(jnp.sum(jnp.where(matches, start_rows[..., None, :], 0), axis=-1)).astype(jnp.int32)
    valid = places < end_rows[..., -1:]
    return (source, (places - begin_at).astype(jnp.int32), valid, matches)

def reference(loader_rows, cotangent, gains, block_rows, block_clip):
    loaders = block_rows.shape[0]
    band_count = block_rows.shape[1]
    capacity = loader_rows.shape[2] // band_count
    row_width = loader_rows.shape[3]
    head_count = gains.shape[1]
    head_size = gains.shape[2]
    length = band_count * capacity
    source, within, valid, matches = locate(block_rows, capacity)
    send_start = (jnp.cumsum(block_rows, axis=0) - block_rows).astype(jnp.int32)
    begin_send = lax.optimization_barrier(jnp.sum(jnp.where(matches, send_start[:, :, None, :], 0), axis=-1)).astype(jnp.int32)
    band_base = (jnp.arange(band_count, dtype=jnp.int32) * capacity)[None, :, None]
    loader_row = jnp.where(valid, band_base + begin_send + within, 0).astype(jnp.int32)
    labels = jnp.where(valid, lax.optimization_barrier(jnp.sum(jnp.where(matches, block_clip[:, None, None, :], 0), axis=-1)), -1).astype(jnp.int32)

    def one_pack(pack_index):
        picked = loader_rows[:, source[pack_index], loader_row[pack_index]]
        keep_mask = valid[pack_index]
        packed = jnp.where(keep_mask[None, :, :, None], picked, jnp.zeros((), loader_rows.dtype)).reshape(3, length, row_width)
        split_rows = packed.reshape(3, length, head_count, head_size).transpose(0, 2, 1, 3).reshape(3, head_count, band_count, capacity, head_size)
        cot_heads = cotangent[pack_index].reshape(length, head_count, head_size).transpose(1, 0, 2).reshape(head_count, band_count, capacity, head_size)
        pack_labels = labels[pack_index]

        def one_head(pack_item):
            queries, key_rows, value_rows, cot_rows, gain_query, gain_key = pack_item
            grad_q, grad_k, grad_v, grad_gq, grad_gk = head_grads(queries, key_rows, value_rows, cot_rows, pack_labels, keep_mask, gain_query, gain_key)
            return (grad_q, grad_k, grad_v, lax.optimization_barrier(jnp.sum(grad_gq, axis=0)), lax.optimization_barrier(jnp.sum(grad_gk, axis=0)))
        grad_q, grad_k, grad_v, grad_gq, grad_gk = lax.map(one_head, (split_rows[0], split_rows[1], split_rows[2], cot_heads, gains[0], gains[1]))
        stacked = jnp.stack([grad_q, grad_k, grad_v]).reshape(3, head_count, length, head_size)
        stacked = stacked.transpose(0, 2, 1, 3).reshape(3, length, row_width)
        return (stacked, jnp.stack([grad_gq, grad_gk]))
    gradients, gain_parts = lax.map(one_pack, jnp.arange(loaders, dtype=jnp.int32))
    return (jnp.transpose(gradients, (1, 0, 2, 3)), lax.optimization_barrier(jnp.sum(gain_parts, axis=0)))
```

```python
import functools
import math

import jax
import jax.numpy as jnp
from jax import lax
from jax.experimental import pallas as pl
from jax.experimental.pallas import tpu as pltpu
from jax.sharding import PartitionSpec as P


epsilon = 1e-06
SLOTS = 3
EXTRA = 16
GROUP = 8


def iota(shape, axis):
    return lax.broadcasted_iota(jnp.int32, shape, axis)


def dot(left, right, left_axis=1, right_axis=0):
    return lax.dot_general(
        left,
        right,
        (((left_axis,), (right_axis,)), ((), ())),
        preferred_element_type=jnp.float32,
    )


def gather_kernel(loaders, bands, capacity, place_ref, table_ref, rows_ref, out_ref, pick_ref, last_ref):
    step = pl.program_id(0)
    lines = loaders * GROUP
    me = place_ref[0]
    my_loader = me // bands
    my_band = me % bands

    @pl.when(step == 0)
    def _():
        table = table_ref[...].astype(jnp.bfloat16)
        peer = iota((lines, loaders * bands), 0) // GROUP
        entry = iota((lines, loaders * bands), 1)
        in_band = (entry % bands) == my_band
        before = jnp.where(in_band & (entry // bands < peer), 1.0, 0.0).astype(jnp.bfloat16)
        same = jnp.where(in_band & (entry // bands == peer), 1.0, 0.0).astype(jnp.bfloat16)
        mine = iota((lines, loaders), 1) == my_loader
        start = jnp.sum(jnp.where(mine, dot(before, table), 0.0), axis=1, keepdims=True).astype(jnp.int32)
        count = jnp.sum(jnp.where(mine, dot(same, table), 0.0), axis=1, keepdims=True).astype(jnp.int32)
        kind = iota((lines, 1), 0) % GROUP
        slot = kind // 3
        column = jnp.where(slot < count, (kind % 3) * capacity + start + slot, -1)
        column_last = jnp.where(count > SLOTS - 1, 2 * capacity + start + (SLOTS - 1), -1)
        lanes = iota((lines, 3 * capacity), 1)
        pick_ref[:lines] = jnp.where(lanes == column, 1.0, 0.0).astype(jnp.bfloat16)
        pick_ref[lines:] = jnp.where(lanes == column_last, 1.0, 0.0).astype(jnp.bfloat16)

    steps = pl.num_programs(0)

    @pl.when(step < steps - 1)
    def _():
        picked = dot(pick_ref[...], rows_ref[...]).astype(jnp.bfloat16)
        out_ref[...] = picked[:lines]
        half = rows_ref.shape[1] // 2
        group = iota((lines, half), 0) % GROUP
        lane = pl.ds(pl.multiple_of((2 * step // GROUP) * half, half), half)
        kept = last_ref[:, lane]
        for part in range(2):
            kept = jnp.where(
                group == (2 * step + part) % GROUP, picked[lines:, part * half : (part + 1) * half], kept
            )
        last_ref[:, lane] = kept

    @pl.when(step == steps - 1)
    def _():
        out_ref[...] = last_ref[...]


def split_kernel(bands, capacity, place_ref, gains_ref, *refs):
    gains = gains_ref[...]
    row = iota((EXTRA, 2 * gains.shape[2]), 0)
    extra = jnp.zeros(row.shape, jnp.float32)
    for kind in range(2):
        line = jnp.concatenate([gains[kind, 0:1], gains[kind, 1:2]], axis=1)
        for part in range(3):
            piece = line.astype(jnp.bfloat16).astype(jnp.float32)
            extra = jnp.where(row == 2 * part + kind, piece, extra)
            line = line - piece
    extra = extra.astype(jnp.bfloat16)
    for shift in range(bands):
        refs[bands + shift][:capacity] = refs[shift][0]
        refs[bands + shift][capacity:] = extra


def attention_kernel(
    loaders, bands, capacity, head_size,
    place_ref, table_ref, clip_ref, rows_ref, last_rows_ref, *refs,
):
    chunk_refs = refs[:bands]
    grad_ref, gain_ref, pick_ref, pick_last_ref, same_ref, cot_ref = refs[bands:]
    step = pl.program_id(0)
    lines = loaders * GROUP
    scale = 1.0 / math.sqrt(head_size)
    me = place_ref[0]
    table_row = table_ref[pl.ds(me, 1), :]
    total = jnp.sum(table_row, axis=1, keepdims=True)
    valid = iota((capacity, 1), 0) < total

    @pl.when(step == 0)
    def _():
        counts = jnp.broadcast_to(table_row, (8, loaders)).astype(jnp.float32).astype(jnp.bfloat16)
        source = iota((loaders, lines), 1) // GROUP
        entry = iota((loaders, lines), 0)
        start = dot(counts, jnp.where(entry < source, 1.0, 0.0).astype(jnp.bfloat16))[:1].astype(jnp.int32)
        count = dot(counts, jnp.where(entry == source, 1.0, 0.0).astype(jnp.bfloat16))[:1].astype(jnp.int32)
        kind = iota((1, lines), 1) % GROUP
        slot = kind // 3
        place = iota((capacity, lines), 0)
        hit = (place == start + slot) & (slot < count)
        for part in range(3):
            pick_ref[part * capacity : (part + 1) * capacity] = jnp.where(
                hit & (kind % 3 == part), 1.0, 0.0
            ).astype(jnp.bfloat16)
        hit_last = (place == start + (SLOTS - 1)) & (count > SLOTS - 1)
        pick_last_ref[...] = jnp.where(hit_last, 1.0, 0.0).astype(jnp.bfloat16)
        clip_row = clip_ref[pl.ds(me // bands, 1), :]
        clip_lines = dot(
            jnp.broadcast_to(clip_row, (8, loaders)).astype(jnp.float32).astype(jnp.bfloat16),
            jnp.where(entry == source, 1.0, 0.0).astype(jnp.bfloat16),
        )[:1].astype(jnp.int32)
        first = kind == 0
        owned = (place >= start) & (place < start + count) & first
        owned = jnp.where(owned, 1.0, 0.0).astype(jnp.bfloat16)
        label_is = jnp.where(iota((16, lines), 0) == clip_lines, 1.0, 0.0).astype(jnp.bfloat16)
        label = dot(owned, label_is, 1, 1)
        label = jnp.where(iota((capacity, 16), 1) == 15, jnp.where(valid, 0.0, 1.0), label)
        label = label.astype(jnp.bfloat16)
        same_ref[...] = dot(label, label, 1, 1)
        for shift in range(bands):
            cot_ref[shift] = chunk_refs[shift][...]

    chunk = cot_ref[(me + bands - step) % bands]
    pieces = chunk[capacity:].astype(jnp.float32)
    gains = pieces[0:2] + pieces[2:4] + pieces[4:6]
    same = same_ref[...] > 0.5
    group = iota((capacity, lines), 1) % GROUP
    pick_last = jnp.where(group == step % GROUP, pick_last_ref[...], jnp.zeros((), jnp.bfloat16))
    packed = dot(pick_ref[...], rows_ref[...])
    queries = packed[:capacity]
    key_rows = packed[capacity : 2 * capacity]
    value_rows = (packed[2 * capacity :] + dot(pick_last, last_rows_ref[...])).astype(jnp.bfloat16)
    cot_rows = jnp.where(valid, chunk[:capacity], jnp.zeros((), jnp.bfloat16))

    def standardize(rows):
        centred = rows - jnp.mean(rows, axis=-1, keepdims=True)
        spread = jnp.mean(centred * centred, axis=-1, keepdims=True)
        factor = lax.rsqrt(spread + epsilon)
        return centred * factor, factor

    for head in range(2):
        lanes = slice(head * head_size, (head + 1) * head_size)
        gain_query = gains[0:1, lanes]
        gain_key = gains[1:2, lanes]
        query_hat, query_factor = standardize(queries[:, lanes])
        key_hat, key_factor = standardize(key_rows[:, lanes])
        qn = (query_hat * gain_query).astype(jnp.bfloat16)
        kn = (key_hat * gain_key).astype(jnp.bfloat16)
        value = value_rows[:, lanes]
        dout = cot_rows[:, lanes]
        weight = jnp.where(same, jnp.exp(dot(qn, kn, 1, 1) * scale), 0.0)
        prob = weight * (1.0 / jnp.sum(weight, axis=-1, keepdims=True))
        prob_b = prob.astype(jnp.bfloat16)
        dprob = dot(dout, value, 1, 1)
        delta = jnp.sum(prob_b.astype(jnp.float32) * dprob, axis=-1, keepdims=True)
        dscore = (prob * (dprob - delta) * scale).astype(jnp.bfloat16)
        dqn = dot(dscore, kn)
        dkn = dot(dscore, qn, 0, 0)
        dvalue = dot(prob_b, dout, 0, 0)
        for part, (grad, hat, factor, gain) in enumerate(
            ((dqn, query_hat, query_factor, gain_query), (dkn, key_hat, key_factor, gain_key))
        ):
            product = grad * hat
            gain_ref[0, 2 * part + head : 2 * part + head + 1, :] = jnp.sum(product, axis=0, keepdims=True)
            scaled = grad * gain
            first = jnp.mean(scaled, axis=-1, keepdims=True)
            second = jnp.mean(product * gain, axis=-1, keepdims=True)
            grad_ref[part, :, lanes] = (factor * (scaled - first - hat * second)).astype(jnp.bfloat16)
        grad_ref[2, :, lanes] = dvalue.astype(jnp.bfloat16)


def shards(loader_rows, cotangent, gains, block_rows, block_clip):
    loaders = lax.axis_size("dp")
    bands = lax.axis_size("seq")
    capacity = loader_rows.shape[2]
    width = loader_rows.shape[3]
    head_size = gains.shape[2]
    lines = loaders * GROUP
    pair = 2 * head_size
    pairs = width // pair
    place = lax.axis_index(("dp", "seq")).astype(jnp.int32).reshape(1)
    table = block_rows.reshape(loaders * bands, loaders)
    smem = pl.BlockSpec(memory_space=pltpu.SMEM)

    gather = pl.pallas_call(
        functools.partial(gather_kernel, loaders, bands, capacity),
        grid=(width // (2 * pair) + 1,),
        in_specs=[
            smem,
            pl.BlockSpec((loaders * bands, loaders), lambda t: (0, 0)),
            pl.BlockSpec((3 * capacity, 2 * pair), lambda t: (0, jnp.minimum(t, width // (2 * pair) - 1))),
        ],
        out_specs=pl.BlockSpec((lines, 2 * pair), lambda t: (0, t)),
        out_shape=jax.ShapeDtypeStruct((lines, width + 2 * pair), jnp.bfloat16),
        scratch_shapes=[
            pltpu.VMEM((2 * lines, 3 * capacity), jnp.bfloat16),
            pltpu.VMEM((lines, 2 * pair), jnp.bfloat16),
        ],
        name="gather_rows",
    )
    with jax.named_scope("gather"):
        outgoing = gather(place, table, loader_rows.reshape(3 * capacity, width))
    with jax.named_scope("row_move"):
        arrived = lax.all_to_all(outgoing, "dp", split_axis=0, concat_axis=0, tiled=True)

    def chunk_map(shift):
        return lambda t, place: ((place[0] + shift) % bands, 0, 0)

    split = pl.pallas_call(
        functools.partial(split_kernel, bands, capacity),
        grid_spec=pltpu.PrefetchScalarGridSpec(
            num_scalar_prefetch=1,
            grid=(1,),
            in_specs=[pl.BlockSpec((2, 2, head_size), lambda t, place: (0, 0, 0))]
            + [pl.BlockSpec((1, capacity, pair), chunk_map(shift)) for shift in range(bands)],
            out_specs=[pl.BlockSpec((capacity + EXTRA, pair), lambda t, place: (0, 0))] * bands,
        ),
        out_shape=[jax.ShapeDtypeStruct((capacity + EXTRA, pair), jnp.bfloat16)] * bands,
        compiler_params=pltpu.CompilerParams(vmem_limit_bytes=8 << 20),
        name="split_cotangent",
    )
    with jax.named_scope("split"):
        chunks = split(place, gains, *([cotangent.reshape(bands, capacity, pair)] * bands))
    with jax.named_scope("cot_move"):
        chunks = [chunks[0]] + [
            lax.ppermute(chunks[shift], "seq", [(j, (j + shift) % bands) for j in range(bands)])
            for shift in range(1, bands)
        ]

    attend = pl.pallas_call(
        functools.partial(attention_kernel, loaders, bands, capacity, head_size),
        grid=(pairs,),
        in_specs=[
            smem,
            pl.BlockSpec((loaders * bands, loaders), lambda t: (0, 0)),
            pl.BlockSpec((loaders, loaders), lambda t: (0, 0)),
            pl.BlockSpec((lines, pair), lambda t: (0, t)),
            pl.BlockSpec((lines, pair), lambda t: (0, pairs + t // GROUP)),
        ]
        + [pl.BlockSpec((capacity + EXTRA, pair), lambda t: (0, 0))] * bands,
        out_specs=[
            pl.BlockSpec((3, capacity, pair), lambda t: (0, 0, t)),
            pl.BlockSpec((1, 4, head_size), lambda t: (t, 0, 0)),
        ],
        out_shape=[
            jax.ShapeDtypeStruct((3, capacity, width), jnp.bfloat16),
            jax.ShapeDtypeStruct((bands, 4, head_size), jnp.float32),
        ],
        scratch_shapes=[
            pltpu.VMEM((3 * capacity, lines), jnp.bfloat16),
            pltpu.VMEM((capacity, lines), jnp.bfloat16),
            pltpu.VMEM((capacity, capacity), jnp.float32),
            pltpu.VMEM((bands, capacity + EXTRA, pair), jnp.bfloat16),
        ],
        compiler_params=pltpu.CompilerParams(vmem_limit_bytes=16 << 20),
        name="attend_pack",
    )
    gradients, gain_parts = attend(place, table, block_clip, arrived, arrived, *chunks)
    by_head = lax.all_to_all(gain_parts, "seq", split_axis=0, concat_axis=0, tiled=True)
    own = jnp.sum(by_head, axis=0, keepdims=True)
    every = lax.all_to_all(
        jnp.broadcast_to(own, (loaders, 4, head_size)), "dp", split_axis=0, concat_axis=0, tiled=True
    )
    gain_total = jnp.sum(every, axis=0).reshape(2, 2, head_size)
    return (gradients[:, None], gain_total)


def solution(mesh):
    in_specs = (P(None, "dp", "seq", None), P("dp", None, "seq"), P(None, "seq", None), P(), P())
    out_specs = (P(None, "dp", "seq", None), P(None, "seq", None))
    return jax.shard_map(shards, mesh=mesh, in_specs=in_specs, out_specs=out_specs, check_vma=False)
```

```python
import functools
import math

import jax
import jax.numpy as jnp
from jax import lax
from jax.experimental import pallas as pl
from jax.experimental.pallas import tpu as pltpu
from jax.sharding import PartitionSpec as P


epsilon = 1e-06
SLOTS = 3
EXTRA = 8
GROUP = 8


def iota(shape, axis):
    return lax.broadcasted_iota(jnp.int32, shape, axis)


def dot(left, right, left_axis=1, right_axis=0):
    return lax.dot_general(
        left,
        right,
        (((left_axis,), (right_axis,)), ((), ())),
        preferred_element_type=jnp.float32,
    )


def gather_kernel(
    loaders, bands, capacity,
    place_ref, table_ref, rows_ref, own_ref, other_ref, pick_ref, pick_last_ref, last_ref,
):
    step = pl.program_id(0)
    steps = pl.num_programs(0)
    lines = loaders * GROUP
    half = rows_ref.shape[1] // 2
    me = place_ref[0]

    @pl.when(step == 0)
    def _():
        my_loader = me // bands
        my_core = my_loader % 2
        column = iota((1, loaders * bands), 1)
        band = column % bands
        target = jnp.where(band == me % bands, column // bands, -1)
        owner = iota((loaders, 1), 0)
        owner = 2 * (owner % (loaders // 2)) + (owner // (loaders // 2) + my_core) % 2
        before = jnp.where((target < owner) & (target >= 0), 1.0, 0.0)
        same = jnp.where(target == owner, 1.0, 0.0)
        table = table_ref[...].astype(jnp.float32).astype(jnp.bfloat16)
        sums = dot(jnp.concatenate([before, same], axis=0).astype(jnp.bfloat16), table)
        sums = jnp.where(iota(sums.shape, 1) == my_loader, sums, 0.0)
        sums = jnp.sum(sums, axis=1, keepdims=True)
        start, count = sums[:loaders].astype(jnp.int32), sums[loaders:].astype(jnp.int32)
        last_column = jnp.where(count > SLOTS - 1, start + (SLOTS - 1), -1)
        pick_last_ref[...] = jnp.where(iota((loaders, capacity), 1) == last_column, 1.0, 0.0).astype(jnp.bfloat16)
        spread = jnp.where(iota((lines, 1), 0) // GROUP == iota((1, loaders), 1), 1.0, 0.0).astype(jnp.bfloat16)
        wide = dot(spread, jnp.concatenate([start, count], axis=1).astype(jnp.float32).astype(jnp.bfloat16))
        start, count = wide[:, 0:1].astype(jnp.int32), wide[:, 1:2].astype(jnp.int32)
        kind = iota((lines, 1), 0) % GROUP
        slot = kind // 3
        line_column = jnp.where(slot < count, (kind - 3 * slot) * capacity + start + slot, -1)
        lanes = iota((lines, 3 * capacity), 1)
        pick_ref[...] = jnp.where(lanes == line_column, 1.0, 0.0).astype(jnp.bfloat16)

    @pl.when(step < steps - 1)
    def _():
        picked = dot(pick_ref[...], rows_ref[...]).astype(jnp.bfloat16)
        own_ref[...] = picked[: lines // 2]
        other_ref[...] = picked[lines // 2 :]
        last = dot(pick_last_ref[...], rows_ref[2 * capacity :])
        for part in range(2):
            group = (2 * step + part) % GROUP
            for low in range(0, half, 128):
                tile = (2 * step // GROUP) * (half // 128) + low // 128
                at = part * half + low
                last_ref[tile, pl.ds(group, loaders, stride=GROUP), :] = last[:, at : at + 128]

    @pl.when(step == steps - 1)
    def _():
        for tile in range(last_ref.shape[0]):
            at = slice(tile * 128, (tile + 1) * 128)
            last = last_ref[tile].astype(jnp.bfloat16)
            own_ref[:, at] = last[: lines // 2]
            other_ref[:, at] = last[lines // 2 :]


def chunk_kernel(capacity, cot_ref, gains_ref, out_ref):
    gains = gains_ref[...]
    row = iota((EXTRA, 2 * gains.shape[2]), 0)
    extra = jnp.zeros(row.shape, jnp.float32)
    for kind in range(2):
        line = jnp.concatenate([gains[kind, 0:1], gains[kind, 1:2]], axis=1)
        for part in range(3):
            piece = line.astype(jnp.bfloat16).astype(jnp.float32)
            extra = jnp.where(row == 2 * part + kind, piece, extra)
            line = line - piece
    extra = extra.astype(jnp.bfloat16)
    for chunk in range(cot_ref.shape[0]):
        out_ref[chunk, :capacity] = cot_ref[chunk]
        out_ref[chunk, capacity:] = extra


def attention_kernel(
    loaders, bands, capacity, head_size,
    place_ref, table_ref, clip_ref, rows_ref, last_rows_ref, chunk_ref,
    grad_ref, gain_ref,
    pick_ref, pick_last_ref, same_ref,
):
    step = pl.program_id(0)
    lines = loaders * GROUP
    scale = 1.0 / math.sqrt(head_size)
    me = place_ref[0]
    my_core = (me // bands) % 2
    table_row = table_ref[pl.ds(me, 1), :]
    total = jnp.sum(table_row, axis=1, keepdims=True)
    valid = iota((capacity, 1), 0) < total

    @pl.when(step == 0)
    def _():
        counts = jnp.broadcast_to(table_row, (8, loaders)).astype(jnp.float32).astype(jnp.bfloat16)
        block = iota((loaders, lines), 1) // GROUP
        source = block - block % 2 + (block % 2 + my_core) % 2
        entry = iota((loaders, lines), 0)
        start = dot(counts, jnp.where(entry < source, 1.0, 0.0).astype(jnp.bfloat16))[:1].astype(jnp.int32)
        count = dot(counts, jnp.where(entry == source, 1.0, 0.0).astype(jnp.bfloat16))[:1].astype(jnp.int32)
        kind = iota((1, lines), 1) % GROUP
        slot = kind // 3
        place = iota((capacity, lines), 0)
        hit = (place == start + slot) & (slot < count)
        for part in range(3):
            pick_ref[part * capacity : (part + 1) * capacity] = jnp.where(
                hit & (kind % 3 == part), 1.0, 0.0
            ).astype(jnp.bfloat16)
        hit_last = (place == start + (SLOTS - 1)) & (count > SLOTS - 1)
        pick_last_ref[...] = jnp.where(hit_last, 1.0, 0.0).astype(jnp.bfloat16)
        clip_row = clip_ref[pl.ds(me // bands, 1), :]
        clip_lines = dot(
            jnp.broadcast_to(clip_row, (8, loaders)).astype(jnp.float32).astype(jnp.bfloat16),
            jnp.where(entry == source, 1.0, 0.0).astype(jnp.bfloat16),
        )[:1].astype(jnp.int32)
        first = kind == 0
        owned = (place >= start) & (place < start + count) & first
        owned = jnp.where(owned, 1.0, 0.0).astype(jnp.bfloat16)
        label_is = jnp.where(iota((16, lines), 0) == clip_lines, 1.0, 0.0).astype(jnp.bfloat16)
        label = dot(owned, label_is, 1, 1)
        label = jnp.where(iota((capacity, 16), 1) == 15, jnp.where(valid, 0.0, 1.0), label)
        label = label.astype(jnp.bfloat16)
        same_ref[...] = dot(label, label, 1, 1)

    same = same_ref[...] > 0.5
    group = iota((capacity, lines), 1) % GROUP
    width = 2 * head_size
    heads = [slice(head * head_size, (head + 1) * head_size) for head in range(2)]
    in_head = iota((width, width), 0) // head_size == iota((width, width), 1) // head_size
    averager = jnp.where(in_head, 1.0 / head_size, 0.0).astype(jnp.bfloat16)
    bfloat = jnp.bfloat16

    def average(rows):
        return dot(rows, averager)

    units = chunk_ref.shape[0]
    pick_last = [
        jnp.where(group == (units * step + unit) % GROUP, pick_last_ref[...], jnp.zeros((), bfloat))
        for unit in range(units)
    ]
    packed = dot(pick_ref[...], rows_ref[...])
    last = dot(jnp.concatenate(pick_last, axis=0), last_rows_ref[...])
    lane = [slice(unit * width, (unit + 1) * width) for unit in range(units)]
    span = [slice(unit * capacity, (unit + 1) * capacity) for unit in range(units)]
    value = [(packed[2 * capacity :, lane[u]] + last[span[u]]).astype(bfloat) for u in range(units)]
    extra = [chunk_ref[u, capacity:].astype(jnp.float32) for u in range(units)]
    gains = [rows[0:2] + rows[2:4] + rows[4:6] for rows in extra]
    dout = [jnp.where(valid, chunk_ref[u, :capacity], jnp.zeros((), bfloat)) for u in range(units)]
    raw = jnp.concatenate(
        [packed[part * capacity : (part + 1) * capacity, lane[u]] for part in range(2) for u in range(units)], axis=0
    )
    centred = raw - average(raw.astype(bfloat))
    factor = lax.rsqrt(average((centred * centred).astype(bfloat)) + epsilon)
    hat = centred * factor
    hats = [[hat[(part * units + u) * capacity :][:capacity] for u in range(units)] for part in range(2)]
    qn = [(hats[0][u] * gains[u][0:1]).astype(bfloat) for u in range(units)]
    kn = [(hats[1][u] * gains[u][1:2]).astype(bfloat) for u in range(units)]
    each = [(u, lanes) for u in range(units) for lanes in heads]
    score = [dot(kn[u][:, lanes], qn[u][:, lanes], 1, 1) for u, lanes in each]
    dprob = [dot(value[u][:, lanes], dout[u][:, lanes], 1, 1) for u, lanes in each]
    weight = [jnp.where(same, jnp.exp(rows * scale), 0.0) for rows in score]
    prob = [rows * (1.0 / jnp.sum(rows, axis=0, keepdims=True)) for rows in weight]
    delta = [jnp.sum(p * d, axis=0, keepdims=True) for p, d in zip(prob, dprob)]
    dscore = [(p * (d - e)).astype(bfloat) for p, d, e in zip(prob, dprob, delta)]
    grads = [
        [dot(dscore[n], kn[u][:, lanes], 0, 0) for n, (u, lanes) in enumerate(each)],
        [dot(dscore[n], qn[u][:, lanes]) for n, (u, lanes) in enumerate(each)],
    ]
    dvalue = [dot(prob[n].astype(bfloat), dout[u][:, lanes]) for n, (u, lanes) in enumerate(each)]
    for n, (u, lanes) in enumerate(each):
        grad_ref[2, :, u * width + lanes.start : u * width + lanes.stop] = dvalue[n].astype(bfloat)
    scaled, seconds = [], []
    for part in range(2):
        for u in range(units):
            grad = jnp.concatenate(grads[part][2 * u : 2 * u + 2], axis=1)
            gain = gains[u][part : part + 1] * scale
            product = grad * hats[part][u]
            total_gain = jnp.sum(product, axis=0, keepdims=True) * scale
            for head, lanes in enumerate(heads):
                gain_ref[u, 2 * part + head : 2 * part + head + 1, :] = total_gain[:, lanes]
            scaled.append(grad * gain)
            seconds.append(product * gain)
    scaled = jnp.concatenate(scaled, axis=0)
    first = average(scaled.astype(bfloat))
    second = average(jnp.concatenate(seconds, axis=0).astype(bfloat))
    result = (factor * (scaled - first - hat * second)).astype(bfloat)
    for part in range(2):
        for u in range(units):
            grad_ref[part, :, lane[u]] = result[(part * units + u) * capacity :][:capacity]


def shards(loader_rows, cotangent, gains, block_rows, block_clip):
    loaders = lax.axis_size("chip") * 2
    bands = lax.axis_size("seq")
    capacity = loader_rows.shape[2]
    width = loader_rows.shape[3]
    head_size = gains.shape[2]
    lines = loaders * GROUP
    pair = 2 * head_size
    pairs = width // pair
    place = lax.axis_index(("chip", "core", "seq")).astype(jnp.int32).reshape(1)
    table = block_rows.reshape(loaders * bands, loaders)
    smem = pl.BlockSpec(memory_space=pltpu.SMEM)

    gather = pl.pallas_call(
        functools.partial(gather_kernel, loaders, bands, capacity),
        grid=(width // (2 * pair) + 1,),
        in_specs=[
            smem,
            pl.BlockSpec((loaders * bands, loaders), lambda t: (0, 0)),
            pl.BlockSpec((3 * capacity, 2 * pair), lambda t: (0, jnp.minimum(t, width // (2 * pair) - 1))),
        ],
        out_specs=[pl.BlockSpec((lines // 2, 2 * pair), lambda t: (0, t))] * 2,
        out_shape=[jax.ShapeDtypeStruct((lines // 2, width + 2 * pair), jnp.bfloat16)] * 2,
        scratch_shapes=[
            pltpu.VMEM((lines, 3 * capacity), jnp.bfloat16),
            pltpu.VMEM((loaders, capacity), jnp.bfloat16),
            pltpu.VMEM((2 * pair // 128, lines, 128), jnp.float32),
        ],
        name="gather_rows",
    )
    pack = pl.pallas_call(
        functools.partial(chunk_kernel, capacity),
        grid=(4,),
        in_specs=[
            pl.BlockSpec((bands // 4, capacity, pair), lambda t: (t, 0, 0)),
            pl.BlockSpec((2, 2, head_size), lambda t: (0, 0, 0)),
        ],
        out_specs=pl.BlockSpec((bands // 4, capacity + EXTRA, pair), lambda t: (t, 0, 0)),
        out_shape=jax.ShapeDtypeStruct((bands, capacity + EXTRA, pair), jnp.bfloat16),
        name="chunk_cotangent",
    )
    chunks = pack(cotangent.reshape(bands, capacity, pair), gains)
    own, other = gather(place, table, loader_rows.reshape(3 * capacity, width))
    other = lax.ppermute(other, "core", [(0, 1), (1, 0)])
    shape = (loaders // 2, 1, GROUP, width + 2 * pair)
    outgoing = jnp.concatenate([own.reshape(shape), other.reshape(shape)], axis=1)

    def move_rows(rows):
        return lax.all_to_all(rows, "chip", split_axis=0, concat_axis=0, tiled=True)

    def move_chunks(chunks):
        return lax.all_to_all(chunks, "seq", split_axis=0, concat_axis=0, tiled=True)

    def rows_first(rows, chunks):
        rows, chunks = lax.optimization_barrier((move_rows(rows), chunks))
        return rows, move_chunks(chunks)

    def chunks_first(rows, chunks):
        rows, chunks = lax.optimization_barrier((rows, move_chunks(chunks)))
        return move_rows(rows), chunks

    arrived, chunks = lax.cond(lax.axis_index("core") == 0, rows_first, chunks_first, outgoing, chunks)
    arrived = arrived.reshape(lines, width + 2 * pair)

    attend = pl.pallas_call(
        functools.partial(attention_kernel, loaders, bands, capacity, head_size),
        grid=(pairs // 4,),
        in_specs=[
            smem,
            pl.BlockSpec((loaders * bands, loaders), lambda t: (0, 0)),
            pl.BlockSpec((loaders, loaders), lambda t: (0, 0)),
            pl.BlockSpec((lines, 4 * pair), lambda t: (0, t)),
            pl.BlockSpec((lines, pair), lambda t: (0, pairs + 4 * t // GROUP)),
            pl.BlockSpec((4, capacity + EXTRA, pair), lambda t: (t, 0, 0)),
        ],
        out_specs=[
            pl.BlockSpec((3, capacity, 4 * pair), lambda t: (0, 0, t)),
            pl.BlockSpec((4, 4, head_size), lambda t: (t, 0, 0)),
        ],
        out_shape=[
            jax.ShapeDtypeStruct((3, capacity, width), jnp.bfloat16),
            jax.ShapeDtypeStruct((bands, 4, head_size), jnp.float32),
        ],
        scratch_shapes=[
            pltpu.VMEM((3 * capacity, lines), jnp.bfloat16),
            pltpu.VMEM((capacity, lines), jnp.bfloat16),
            pltpu.VMEM((capacity, capacity), jnp.float32),
        ],
        compiler_params=pltpu.CompilerParams(vmem_limit_bytes=16 << 20),
        name="attend_pack",
    )
    gradients, gain_parts = attend(place, table, block_clip, arrived, arrived, chunks)
    by_head = lax.all_to_all(gain_parts, "seq", split_axis=0, concat_axis=0, tiled=True)
    mine = jnp.sum(by_head, axis=0, keepdims=True)
    every = lax.all_to_all(
        jnp.broadcast_to(mine, (loaders, 4, head_size)), ("chip", "core"), split_axis=0, concat_axis=0, tiled=True
    )
    gain_total = jnp.sum(every, axis=0).reshape(2, 2, head_size)
    return (gradients[:, None], gain_total)


def solution(mesh):
    chips, bands = mesh.devices.shape[0] // 2, mesh.devices.shape[1]
    mesh = jax.sharding.Mesh(mesh.devices.reshape(chips, 2, bands), ("chip", "core", "seq"))
    dp = ("chip", "core")
    in_specs = (P(None, dp, "seq", None), P(dp, None, "seq"), P(None, "seq", None), P(), P())
    out_specs = (P(None, dp, "seq", None), P(None, "seq", None))
    return jax.shard_map(shards, mesh=mesh, in_specs=in_specs, out_specs=out_specs, check_vma=False)
```

```python
import functools
import math

import jax
import jax.numpy as jnp
from jax import lax
from jax.experimental import pallas as pl
from jax.experimental.pallas import tpu as pltpu
from jax.sharding import PartitionSpec as P


epsilon = 1e-06
SLOTS = 3
EXTRA = 8
GROUP = 8


def iota(shape, axis):
    return lax.broadcasted_iota(jnp.int32, shape, axis)


def dot(left, right, left_axis=1, right_axis=0):
    return lax.dot_general(
        left,
        right,
        (((left_axis,), (right_axis,)), ((), ())),
        preferred_element_type=jnp.float32,
    )


def gather_kernel(
    flip, loaders, bands, capacity, place_ref, table_ref, rows_ref, out_ref, pick_ref, pick_last_ref, last_ref
):
    peers = loaders // 2
    lines = peers * GROUP
    half = 128 * last_ref.shape[0] // 2
    steps = rows_ref.shape[1] // (2 * half)
    me = place_ref[0]
    my_loader = me // bands
    column = iota((1, loaders * bands), 1)
    target = jnp.where(column % bands == me % bands, column // bands, -1)
    owner = 2 * iota((peers, 1), 0) + (my_loader + flip) % 2
    before = jnp.where((target < owner) & (target >= 0), 1.0, 0.0)
    same = jnp.where(target == owner, 1.0, 0.0)
    table = table_ref[...].astype(jnp.float32).astype(jnp.bfloat16)
    sums = dot(jnp.concatenate([before, same], axis=0).astype(jnp.bfloat16), table)
    sums = jnp.sum(jnp.where(iota(sums.shape, 1) == my_loader, sums, 0.0), axis=1, keepdims=True)
    start, count = sums[:peers].astype(jnp.int32), sums[peers:].astype(jnp.int32)
    last_column = jnp.where(count > SLOTS - 1, start + (SLOTS - 1), -1)
    pick_last_ref[...] = jnp.where(iota((peers, capacity), 1) == last_column, 1.0, 0.0).astype(jnp.bfloat16)
    spread = jnp.where(iota((lines, 1), 0) // GROUP == iota((1, peers), 1), 1.0, 0.0).astype(jnp.bfloat16)
    wide = dot(spread, jnp.concatenate([start, count], axis=1).astype(jnp.float32).astype(jnp.bfloat16))
    start, count = wide[:, 0:1].astype(jnp.int32), wide[:, 1:2].astype(jnp.int32)
    kind = iota((lines, 1), 0) % GROUP
    slot = kind // 3
    line_column = jnp.where(slot < count, (kind - 3 * slot) * capacity + start + slot, -1)
    lanes = iota((lines, 3 * capacity), 1)
    pick_ref[...] = jnp.where(lanes == line_column, 1.0, 0.0).astype(jnp.bfloat16)
    for step in range(steps):
        at = slice(2 * step * half, 2 * (step + 1) * half)
        out_ref[:, at] = dot(pick_ref[...], rows_ref[:, at]).astype(jnp.bfloat16)
        last = dot(pick_last_ref[...], rows_ref[2 * capacity :, at])
        for part in range(2):
            unit = 2 * step + part
            for low in range(0, half, 128):
                tile = (unit // GROUP) * (half // 128) + low // 128
                lane = part * half + low
                last_ref[tile, pl.ds(unit % GROUP, peers, stride=GROUP), :] = last[:, lane : lane + 128]
    for tile in range(last_ref.shape[0]):
        at = slice(rows_ref.shape[1] + tile * 128, rows_ref.shape[1] + (tile + 1) * 128)
        out_ref[:, at] = last_ref[tile].astype(jnp.bfloat16)


def chunk_kernel(capacity, cot_ref, gains_ref, out_ref):
    head_size = out_ref.shape[2]
    row = iota((EXTRA, head_size), 0)
    extra = jnp.zeros(row.shape, jnp.float32)
    for kind in range(2):
        for head in range(2):
            line = gains_ref[kind, head : head + 1, :]
            for part in range(2):
                piece = line.astype(jnp.bfloat16).astype(jnp.float32)
                extra = jnp.where(row == 4 * part + 2 * kind + head, piece, extra)
                line = line - piece
    extra = extra.astype(jnp.bfloat16)
    for chunk in range(cot_ref.shape[0]):
        for head in range(2):
            lanes = slice(head * head_size, (head + 1) * head_size)
            out_ref[chunk, head * capacity : (head + 1) * capacity] = cot_ref[chunk, :, lanes]
        out_ref[chunk, 2 * capacity :] = extra


def attention_kernel(
    loaders, bands, capacity, head_size,
    place_ref, table_ref, clip_ref, rows_ref, chunk_ref,
    grad_ref, gain_ref,
    pick_ref, pick_last_ref, same_ref,
):
    step = pl.program_id(0)
    lines = loaders * GROUP
    scale = 1.0 / math.sqrt(head_size)
    me = place_ref[0]
    my_core = (me // bands) % 2
    table_row = table_ref[pl.ds(me, 1), :]
    total = jnp.sum(table_row, axis=1, keepdims=True)
    valid = iota((capacity, 1), 0) < total

    @pl.when(step == 0)
    def _():
        counts = jnp.broadcast_to(table_row, (8, loaders)).astype(jnp.float32).astype(jnp.bfloat16)
        block = iota((loaders, lines), 1) // GROUP
        source = block - block % 2 + (block % 2 + my_core) % 2
        entry = iota((loaders, lines), 0)
        start = dot(counts, jnp.where(entry < source, 1.0, 0.0).astype(jnp.bfloat16))[:1].astype(jnp.int32)
        count = dot(counts, jnp.where(entry == source, 1.0, 0.0).astype(jnp.bfloat16))[:1].astype(jnp.int32)
        kind = iota((1, lines), 1) % GROUP
        slot = kind // 3
        place = iota((capacity, lines), 0)
        hit = (place == start + slot) & (slot < count)
        for part in range(3):
            pick_ref[part * capacity : (part + 1) * capacity] = jnp.where(
                hit & (kind % 3 == part), 1.0, 0.0
            ).astype(jnp.bfloat16)
        hit_last = (place == start + (SLOTS - 1)) & (count > SLOTS - 1)
        pick_last_ref[...] = jnp.where(hit_last, 1.0, 0.0).astype(jnp.bfloat16)
        clip_row = clip_ref[pl.ds(me // bands, 1), :]
        clip_lines = dot(
            jnp.broadcast_to(clip_row, (8, loaders)).astype(jnp.float32).astype(jnp.bfloat16),
            jnp.where(entry == source, 1.0, 0.0).astype(jnp.bfloat16),
        )[:1].astype(jnp.int32)
        first = kind == 0
        owned = (place >= start) & (place < start + count) & first
        owned = jnp.where(owned, 1.0, 0.0).astype(jnp.bfloat16)
        label_is = jnp.where(iota((16, lines), 0) == clip_lines, 1.0, 0.0).astype(jnp.bfloat16)
        label = dot(owned, label_is, 1, 1)
        label = jnp.where(iota((capacity, 16), 1) == 15, jnp.where(valid, 0.0, 1.0), label)
        label = label.astype(jnp.bfloat16)
        same_ref[...] = dot(label, label, 1, 1)

    same = same_ref[...] > 0.5
    group = iota((capacity, lines), 1) % GROUP
    width = 2 * head_size
    heads = [slice(head * head_size, (head + 1) * head_size) for head in range(2)]
    in_head = iota((width, width), 0) // head_size == iota((width, width), 1) // head_size
    averager = jnp.where(in_head, 1.0 / head_size, 0.0).astype(jnp.bfloat16)
    bfloat = jnp.bfloat16

    def average(rows):
        return dot(rows, averager)

    units = gain_ref.shape[0]
    base = units * step
    features = chunk_ref.shape[0] * width
    here = pl.ds(pl.multiple_of(base * width, units * width), units * width)
    last_here = pl.ds(pl.multiple_of(features + base // GROUP * width, width), width)
    pick_last = [
        jnp.where(group == (base + unit) % GROUP, pick_last_ref[...], jnp.zeros((), bfloat))
        for unit in range(units)
    ]
    packed = dot(pick_ref[...], rows_ref[:, here])
    last = dot(jnp.concatenate(pick_last, axis=0), rows_ref[:, last_here])
    lane = [slice(unit * width, (unit + 1) * width) for unit in range(units)]
    span = [slice(unit * capacity, (unit + 1) * capacity) for unit in range(units)]
    value = [(packed[2 * capacity :, lane[u]] + last[span[u]]).astype(bfloat) for u in range(units)]
    extra = [chunk_ref[base + u, 2 * capacity :].astype(jnp.float32) for u in range(units)]
    extra = [rows[0:4] + rows[4:8] for rows in extra]
    gains = [
        jnp.concatenate(
            [jnp.concatenate([rows[2 * kind : 2 * kind + 1], rows[2 * kind + 1 : 2 * kind + 2]], axis=1) for kind in range(2)],
            axis=0,
        )
        for rows in extra
    ]
    dout = [
        jnp.where(valid, chunk_ref[base + u, head * capacity : (head + 1) * capacity], jnp.zeros((), bfloat))
        for u in range(units)
        for head in range(2)
    ]
    raw = jnp.concatenate(
        [packed[part * capacity : (part + 1) * capacity, lane[u]] for part in range(2) for u in range(units)], axis=0
    )
    centred = raw - average(raw.astype(bfloat))
    factor = lax.rsqrt(average((centred * centred).astype(bfloat)) + epsilon)
    hat = centred * factor
    hats = [[hat[(part * units + u) * capacity :][:capacity] for u in range(units)] for part in range(2)]
    qn = [(hats[0][u] * gains[u][0:1]).astype(bfloat) for u in range(units)]
    kn = [(hats[1][u] * gains[u][1:2]).astype(bfloat) for u in range(units)]
    each = [(u, lanes) for u in range(units) for lanes in heads]
    score = [dot(kn[u][:, lanes], qn[u][:, lanes], 1, 1) for u, lanes in each]
    dprob = [dot(value[u][:, lanes], dout[n], 1, 1) for n, (u, lanes) in enumerate(each)]
    weight = [jnp.where(same, jnp.exp(rows * scale), 0.0) for rows in score]
    prob = [rows * (1.0 / jnp.sum(rows, axis=0, keepdims=True)) for rows in weight]
    delta = [jnp.sum(p * d, axis=0, keepdims=True) for p, d in zip(prob, dprob)]
    dscore = [(p * (d - e)).astype(bfloat) for p, d, e in zip(prob, dprob, delta)]
    grads = [
        [dot(dscore[n], kn[u][:, lanes], 0, 0) for n, (u, lanes) in enumerate(each)],
        [dot(dscore[n], qn[u][:, lanes]) for n, (u, lanes) in enumerate(each)],
    ]
    dvalue = [dot(prob[n].astype(bfloat), dout[n]) for n in range(len(each))]
    for n, (u, lanes) in enumerate(each):
        grad_ref[2, :, u * width + lanes.start : u * width + lanes.stop] = dvalue[n].astype(bfloat)
    scaled, seconds = [], []
    for part in range(2):
        for u in range(units):
            grad = jnp.concatenate(grads[part][2 * u : 2 * u + 2], axis=1)
            gain = gains[u][part : part + 1] * scale
            product = grad * hats[part][u]
            total_gain = jnp.sum(product, axis=0, keepdims=True) * scale
            for head, lanes in enumerate(heads):
                gain_ref[u, 2 * part + head : 2 * part + head + 1, :] = total_gain[:, lanes]
            scaled.append(grad * gain)
            seconds.append(product * gain)
    scaled = jnp.concatenate(scaled, axis=0)
    first = average(scaled.astype(bfloat))
    second = average(jnp.concatenate(seconds, axis=0).astype(bfloat))
    result = (factor * (scaled - first - hat * second)).astype(bfloat)
    for part in range(2):
        for u in range(units):
            grad_ref[part, :, lane[u]] = result[(part * units + u) * capacity :][:capacity]


def shards(loader_rows, cotangent, gains, block_rows, block_clip):
    loaders = lax.axis_size("chip") * 2
    bands = lax.axis_size("seq")
    capacity = loader_rows.shape[2]
    width = loader_rows.shape[3]
    head_size = gains.shape[2]
    lines = loaders * GROUP
    pair = 2 * head_size
    pairs = width // pair
    place = lax.axis_index(("chip", "core", "seq")).astype(jnp.int32).reshape(1)
    table = block_rows.reshape(loaders * bands, loaders)
    smem = pl.BlockSpec(memory_space=pltpu.SMEM)
    vmem = pl.BlockSpec(memory_space=pltpu.VMEM)

    vmem = pl.BlockSpec(memory_space=pltpu.VMEM)
    def gather(flip):
        return pl.pallas_call(
            functools.partial(gather_kernel, flip, loaders, bands, capacity),
            in_specs=[smem, vmem, vmem],
            out_specs=vmem,
            out_shape=jax.ShapeDtypeStruct((lines // 2, width + 2 * pair), jnp.bfloat16),
            scratch_shapes=[
                pltpu.VMEM((lines // 2, 3 * capacity), jnp.bfloat16),
                pltpu.VMEM((loaders // 2, capacity), jnp.bfloat16),
                pltpu.VMEM((2 * pair // 128, lines // 2, 128), jnp.float32),
            ],
            compiler_params=pltpu.CompilerParams(vmem_limit_bytes=8 << 20),
            cost_estimate=pl.CostEstimate(flops=300_000_000, bytes_accessed=3_000_000, transcendentals=0),
            name="gather_rows" if flip else "gather_own",
        )(place, table, loader_rows.reshape(3 * capacity, width))

    pack = pl.pallas_call(
        functools.partial(chunk_kernel, capacity),
        in_specs=[vmem, vmem],
        out_specs=vmem,
        out_shape=jax.ShapeDtypeStruct((bands, 2 * capacity + EXTRA, head_size), jnp.bfloat16),
        compiler_params=pltpu.CompilerParams(vmem_limit_bytes=8 << 20),
        name="chunk_cotangent",
    )
    chunks = pack(cotangent.reshape(bands, capacity, pair), gains)
    other = gather(1)
    other = lax.ppermute(other, "core", [(0, 1), (1, 0)])
    own = gather(0)
    shape = (loaders // 2, 1, GROUP, width + 2 * pair)
    outgoing = jnp.concatenate([own.reshape(shape), other.reshape(shape)], axis=1)

    def move_rows(rows):
        return lax.all_to_all(rows, "chip", split_axis=0, concat_axis=0, tiled=True)

    def move_chunks(chunks):
        return lax.all_to_all(chunks, "seq", split_axis=0, concat_axis=0, tiled=True)

    def rows_first(rows, chunks):
        rows, chunks = lax.optimization_barrier((move_rows(rows), chunks))
        return rows, move_chunks(chunks)

    def chunks_first(rows, chunks):
        rows, chunks = lax.optimization_barrier((rows, move_chunks(chunks)))
        return move_rows(rows), chunks

    arrived, chunks = lax.cond(lax.axis_index("core") == 0, rows_first, chunks_first, outgoing, chunks)
    arrived = arrived.reshape(lines, width + 2 * pair)

    attend = pl.pallas_call(
        functools.partial(attention_kernel, loaders, bands, capacity, head_size),
        grid=(pairs // 4,),
        in_specs=[
            smem,
            pl.BlockSpec((loaders * bands, loaders), lambda t: (0, 0)),
            pl.BlockSpec((loaders, loaders), lambda t: (0, 0)),
            vmem,
            vmem,
        ],
        out_specs=[
            pl.BlockSpec((3, capacity, 4 * pair), lambda t: (0, 0, t)),
            pl.BlockSpec((4, 4, head_size), lambda t: (t, 0, 0)),
        ],
        out_shape=[
            jax.ShapeDtypeStruct((3, capacity, width), jnp.bfloat16),
            jax.ShapeDtypeStruct((bands, 4, head_size), jnp.float32),
        ],
        scratch_shapes=[
            pltpu.VMEM((3 * capacity, lines), jnp.bfloat16),
            pltpu.VMEM((capacity, lines), jnp.bfloat16),
            pltpu.VMEM((capacity, capacity), jnp.float32),
        ],
        compiler_params=pltpu.CompilerParams(vmem_limit_bytes=16 << 20),
        name="attend_pack",
    )
    gradients, gain_parts = attend(place, table, block_clip, arrived, chunks)
    by_head = lax.all_to_all(gain_parts, "seq", split_axis=0, concat_axis=0, tiled=True)
    mine = jnp.sum(by_head, axis=0, keepdims=True)
    every = lax.all_to_all(
        jnp.broadcast_to(mine, (loaders, 4, head_size)), ("chip", "core"), split_axis=0, concat_axis=0, tiled=True
    )
    gain_total = jnp.sum(every, axis=0).reshape(2, 2, head_size)
    return (gradients[:, None], gain_total)


def solution(mesh):
    chips, bands = mesh.devices.shape[0] // 2, mesh.devices.shape[1]
    mesh = jax.sharding.Mesh(mesh.devices.reshape(chips, 2, bands), ("chip", "core", "seq"))
    dp = ("chip", "core")
    in_specs = (P(None, dp, "seq", None), P(dp, None, "seq"), P(None, "seq", None), P(), P())
    out_specs = (P(None, dp, "seq", None), P(None, "seq", None))
    return jax.shard_map(shards, mesh=mesh, in_specs=in_specs, out_specs=out_specs, check_vma=False)
```

```python
import functools
import math

import jax
import jax.numpy as jnp
from jax import lax
from jax.experimental import pallas as pl
from jax.experimental.pallas import tpu as pltpu
from jax.sharding import PartitionSpec as P


epsilon = 1e-06
SLOTS = 3
EXTRA = 8
GROUP = 8


def iota(shape, axis):
    return lax.broadcasted_iota(jnp.int32, shape, axis)


def dot(left, right, left_axis=1, right_axis=0):
    return lax.dot_general(
        left,
        right,
        (((left_axis,), (right_axis,)), ((), ())),
        preferred_element_type=jnp.float32,
    )


def gather_kernel(
    flip, loaders, bands, capacity, place_ref, table_ref, rows_ref, out_ref, pick_ref, pick_last_ref, last_ref
):
    peers = loaders // 2
    lines = peers * GROUP
    half = 128 * last_ref.shape[0] // 2
    steps = rows_ref.shape[1] // (2 * half)
    me = place_ref[0]
    my_loader = me // bands
    column = iota((1, loaders * bands), 1)
    target = jnp.where(column % bands == me % bands, column // bands, -1)
    owner = 2 * iota((peers, 1), 0) + (my_loader + flip) % 2
    before = jnp.where((target < owner) & (target >= 0), 1.0, 0.0)
    same = jnp.where(target == owner, 1.0, 0.0)
    table = table_ref[...].astype(jnp.float32).astype(jnp.bfloat16)
    sums = dot(jnp.concatenate([before, same], axis=0).astype(jnp.bfloat16), table)
    sums = jnp.sum(jnp.where(iota(sums.shape, 1) == my_loader, sums, 0.0), axis=1, keepdims=True)
    start, count = sums[:peers].astype(jnp.int32), sums[peers:].astype(jnp.int32)
    last_column = jnp.where(count > SLOTS - 1, start + (SLOTS - 1), -1)
    pick_last_ref[...] = jnp.where(iota((peers, capacity), 1) == last_column, 1.0, 0.0).astype(jnp.bfloat16)
    spread = jnp.where(iota((lines, 1), 0) // GROUP == iota((1, peers), 1), 1.0, 0.0).astype(jnp.bfloat16)
    wide = dot(spread, jnp.concatenate([start, count], axis=1).astype(jnp.float32).astype(jnp.bfloat16))
    start, count = wide[:, 0:1].astype(jnp.int32), wide[:, 1:2].astype(jnp.int32)
    kind = iota((lines, 1), 0) % GROUP
    slot = kind // 3
    line_column = jnp.where(slot < count, (kind - 3 * slot) * capacity + start + slot, -1)
    lanes = iota((lines, 3 * capacity), 1)
    pick_ref[...] = jnp.where(lanes == line_column, 1.0, 0.0).astype(jnp.bfloat16)
    for step in range(steps):
        at = slice(2 * step * half, 2 * (step + 1) * half)
        out_ref[:, at] = dot(pick_ref[...], rows_ref[:, at]).astype(jnp.bfloat16)
        last = dot(pick_last_ref[...], rows_ref[2 * capacity :, at])
        for part in range(2):
            unit = 2 * step + part
            for low in range(0, half, 128):
                tile = (unit // GROUP) * (half // 128) + low // 128
                lane = part * half + low
                last_ref[tile, pl.ds(unit % GROUP, peers, stride=GROUP), :] = last[:, lane : lane + 128]
    for tile in range(last_ref.shape[0]):
        at = slice(rows_ref.shape[1] + tile * 128, rows_ref.shape[1] + (tile + 1) * 128)
        out_ref[:, at] = last_ref[tile].astype(jnp.bfloat16)


def chunk_kernel(capacity, cot_ref, gains_ref, out_ref):
    head_size = out_ref.shape[2]
    row = iota((EXTRA, head_size), 0)
    extra = jnp.zeros(row.shape, jnp.float32)
    for kind in range(2):
        for head in range(2):
            line = gains_ref[kind, head : head + 1, :]
            for part in range(2):
                piece = line.astype(jnp.bfloat16).astype(jnp.float32)
                extra = jnp.where(row == 4 * part + 2 * kind + head, piece, extra)
                line = line - piece
    extra = extra.astype(jnp.bfloat16)
    for chunk in range(cot_ref.shape[0]):
        for head in range(2):
            lanes = slice(head * head_size, (head + 1) * head_size)
            out_ref[chunk, head * capacity : (head + 1) * capacity] = cot_ref[chunk, :, lanes]
        out_ref[chunk, 2 * capacity :] = extra


def attention_kernel(
    loaders, bands, capacity, head_size,
    place_ref, table_ref, clip_ref, rows_ref, chunk_ref,
    grad_ref, gain_ref,
    pick_ref, pick_last_ref, same_ref,
):
    step = pl.program_id(0)
    lines = loaders * GROUP
    scale = 1.0 / math.sqrt(head_size)
    me = place_ref[0]
    my_core = (me // bands) % 2
    table_row = table_ref[pl.ds(me, 1), :]
    total = jnp.sum(table_row, axis=1, keepdims=True)
    valid = iota((capacity, 1), 0) < total

    @pl.when(step == 0)
    def _():
        counts = jnp.broadcast_to(table_row, (8, loaders)).astype(jnp.float32).astype(jnp.bfloat16)
        block = iota((loaders, lines), 1) // GROUP
        source = block - block % 2 + (block % 2 + my_core) % 2
        entry = iota((loaders, lines), 0)
        start = dot(counts, jnp.where(entry < source, 1.0, 0.0).astype(jnp.bfloat16))[:1].astype(jnp.int32)
        count = dot(counts, jnp.where(entry == source, 1.0, 0.0).astype(jnp.bfloat16))[:1].astype(jnp.int32)
        kind = iota((1, lines), 1) % GROUP
        slot = kind // 3
        place = iota((capacity, lines), 0)
        hit = (place == start + slot) & (slot < count)
        for part in range(3):
            pick_ref[part * capacity : (part + 1) * capacity] = jnp.where(
                hit & (kind % 3 == part), 1.0, 0.0
            ).astype(jnp.bfloat16)
        hit_last = (place == start + (SLOTS - 1)) & (count > SLOTS - 1)
        pick_last_ref[...] = jnp.where(hit_last, 1.0, 0.0).astype(jnp.bfloat16)
        clip_row = clip_ref[pl.ds(me // bands, 1), :]
        clip_lines = dot(
            jnp.broadcast_to(clip_row, (8, loaders)).astype(jnp.float32).astype(jnp.bfloat16),
            jnp.where(entry == source, 1.0, 0.0).astype(jnp.bfloat16),
        )[:1].astype(jnp.int32)
        first = kind == 0
        owned = (place >= start) & (place < start + count) & first
        owned = jnp.where(owned, 1.0, 0.0).astype(jnp.bfloat16)
        label_is = jnp.where(iota((16, lines), 0) == clip_lines, 1.0, 0.0).astype(jnp.bfloat16)
        label = dot(owned, label_is, 1, 1)
        label = jnp.where(iota((capacity, 16), 1) == 15, jnp.where(valid, 0.0, 1.0), label)
        label = label.astype(jnp.bfloat16)
        same_ref[...] = dot(label, label, 1, 1)

    same = same_ref[...] > 0.5
    group = iota((capacity, lines), 1) % GROUP
    width = 2 * head_size
    heads = [slice(head * head_size, (head + 1) * head_size) for head in range(2)]
    in_head = iota((width, width), 0) // head_size == iota((width, width), 1) // head_size
    averager = jnp.where(in_head, 1.0 / head_size, 0.0).astype(jnp.bfloat16)
    bfloat = jnp.bfloat16

    def average(rows):
        return dot(rows, averager)

    def lane_average(rows):
        means = [jnp.mean(rows[:, lanes], axis=1, keepdims=True) for lanes in heads]
        return jnp.concatenate([jnp.broadcast_to(m, (rows.shape[0], head_size)) for m in means], axis=1)

    units = gain_ref.shape[0]
    base = units * step
    features = chunk_ref.shape[0] * width
    here = pl.ds(pl.multiple_of(base * width, units * width), units * width)
    last_here = pl.ds(pl.multiple_of(features + base // GROUP * width, width), width)
    pick_last = [
        jnp.where(group == (base + unit) % GROUP, pick_last_ref[...], jnp.zeros((), bfloat))
        for unit in range(units)
    ]
    packed = dot(pick_ref[...], rows_ref[:, here])
    last = dot(jnp.concatenate(pick_last, axis=0), rows_ref[:, last_here])
    lane = [slice(unit * width, (unit + 1) * width) for unit in range(units)]
    span = [slice(unit * capacity, (unit + 1) * capacity) for unit in range(units)]
    value = [(packed[2 * capacity :, lane[u]] + last[span[u]]).astype(bfloat) for u in range(units)]
    extra = [chunk_ref[base + u, 2 * capacity :].astype(jnp.float32) for u in range(units)]
    extra = [rows[0:4] + rows[4:8] for rows in extra]
    gains = [
        jnp.concatenate(
            [jnp.concatenate([rows[2 * kind : 2 * kind + 1], rows[2 * kind + 1 : 2 * kind + 2]], axis=1) for kind in range(2)],
            axis=0,
        )
        for rows in extra
    ]
    dout = [
        jnp.where(valid, chunk_ref[base + u, head * capacity : (head + 1) * capacity], jnp.zeros((), bfloat))
        for u in range(units)
        for head in range(2)
    ]
    raw = jnp.concatenate(
        [packed[part * capacity : (part + 1) * capacity, lane[u]] for part in range(2) for u in range(units)], axis=0
    )
    centred = raw - average(raw.astype(bfloat))
    factor = lax.rsqrt(lane_average(centred * centred) + epsilon)
    hat = centred * factor
    hats = [[hat[(part * units + u) * capacity :][:capacity] for u in range(units)] for part in range(2)]
    qn = [(hats[0][u] * gains[u][0:1]).astype(bfloat) for u in range(units)]
    kn = [(hats[1][u] * gains[u][1:2]).astype(bfloat) for u in range(units)]
    each = [(u, lanes) for u in range(units) for lanes in heads]
    score = [dot(kn[u][:, lanes], qn[u][:, lanes], 1, 1) for u, lanes in each]
    dprob = [dot(value[u][:, lanes], dout[n], 1, 1) for n, (u, lanes) in enumerate(each)]
    weight = [jnp.where(same, jnp.exp(rows * scale), 0.0) for rows in score]
    prob = [rows * (1.0 / jnp.sum(rows, axis=0, keepdims=True)) for rows in weight]
    delta = [jnp.sum(p * d, axis=0, keepdims=True) for p, d in zip(prob, dprob)]
    dscore = [(p * (d - e)).astype(bfloat) for p, d, e in zip(prob, dprob, delta)]
    grads = [
        [dot(dscore[n], kn[u][:, lanes], 0, 0) for n, (u, lanes) in enumerate(each)],
        [dot(dscore[n], qn[u][:, lanes]) for n, (u, lanes) in enumerate(each)],
    ]
    dvalue = [dot(prob[n].astype(bfloat), dout[n]) for n in range(len(each))]
    for n, (u, lanes) in enumerate(each):
        grad_ref[2, :, u * width + lanes.start : u * width + lanes.stop] = dvalue[n].astype(bfloat)
    scaled, seconds = [], []
    for part in range(2):
        for u in range(units):
            grad = jnp.concatenate(grads[part][2 * u : 2 * u + 2], axis=1)
            gain = gains[u][part : part + 1] * scale
            product = grad * hats[part][u]
            total_gain = jnp.sum(product, axis=0, keepdims=True) * scale
            for head, lanes in enumerate(heads):
                gain_ref[u, 2 * part + head : 2 * part + head + 1, :] = total_gain[:, lanes]
            scaled.append(grad * gain)
            seconds.append(product * gain)
    scaled = jnp.concatenate(scaled, axis=0)
    first = lane_average(scaled)
    second = average(jnp.concatenate(seconds, axis=0).astype(bfloat))
    result = (factor * (scaled - first - hat * second)).astype(bfloat)
    for part in range(2):
        for u in range(units):
            grad_ref[part, :, lane[u]] = result[(part * units + u) * capacity :][:capacity]


def shards(loader_rows, cotangent, gains, block_rows, block_clip):
    loaders = lax.axis_size("chip") * 2
    bands = lax.axis_size("seq")
    capacity = loader_rows.shape[2]
    width = loader_rows.shape[3]
    head_size = gains.shape[2]
    lines = loaders * GROUP
    pair = 2 * head_size
    pairs = width // pair
    place = lax.axis_index(("chip", "core", "seq")).astype(jnp.int32).reshape(1)
    table = block_rows.reshape(loaders * bands, loaders)
    smem = pl.BlockSpec(memory_space=pltpu.SMEM)
    vmem = pl.BlockSpec(memory_space=pltpu.VMEM)

    vmem = pl.BlockSpec(memory_space=pltpu.VMEM)
    def gather(flip):
        return pl.pallas_call(
            functools.partial(gather_kernel, flip, loaders, bands, capacity),
            in_specs=[smem, vmem, vmem],
            out_specs=vmem,
            out_shape=jax.ShapeDtypeStruct((lines // 2, width + 2 * pair), jnp.bfloat16),
            scratch_shapes=[
                pltpu.VMEM((lines // 2, 3 * capacity), jnp.bfloat16),
                pltpu.VMEM((loaders // 2, capacity), jnp.bfloat16),
                pltpu.VMEM((2 * pair // 128, lines // 2, 128), jnp.float32),
            ],
            compiler_params=pltpu.CompilerParams(vmem_limit_bytes=8 << 20),
            cost_estimate=pl.CostEstimate(flops=300_000_000, bytes_accessed=3_000_000, transcendentals=0),
            name="gather_rows" if flip else "gather_own",
        )(place, table, loader_rows.reshape(3 * capacity, width))

    pack = pl.pallas_call(
        functools.partial(chunk_kernel, capacity),
        in_specs=[vmem, vmem],
        out_specs=vmem,
        out_shape=jax.ShapeDtypeStruct((bands, 2 * capacity + EXTRA, head_size), jnp.bfloat16),
        compiler_params=pltpu.CompilerParams(vmem_limit_bytes=8 << 20),
        name="chunk_cotangent",
    )
    chunks = pack(cotangent.reshape(bands, capacity, pair), gains)
    other = gather(1)
    other = lax.ppermute(other, "core", [(0, 1), (1, 0)])
    own = gather(0)
    shape = (loaders // 2, 1, GROUP, width + 2 * pair)
    outgoing = jnp.concatenate([own.reshape(shape), other.reshape(shape)], axis=1)

    def move_rows(rows):
        return lax.all_to_all(rows, "chip", split_axis=0, concat_axis=0, tiled=True)

    def move_chunks(chunks):
        return lax.all_to_all(chunks, "seq", split_axis=0, concat_axis=0, tiled=True)

    def rows_first(rows, chunks):
        rows, chunks = lax.optimization_barrier((move_rows(rows), chunks))
        return rows, move_chunks(chunks)

    def chunks_first(rows, chunks):
        rows, chunks = lax.optimization_barrier((rows, move_chunks(chunks)))
        return move_rows(rows), chunks

    arrived, chunks = lax.cond(lax.axis_index("core") == 0, rows_first, chunks_first, outgoing, chunks)
    arrived = arrived.reshape(lines, width + 2 * pair)

    attend = pl.pallas_call(
        functools.partial(attention_kernel, loaders, bands, capacity, head_size),
        grid=(pairs // 8,),
        in_specs=[
            smem,
            pl.BlockSpec((loaders * bands, loaders), lambda t: (0, 0)),
            pl.BlockSpec((loaders, loaders), lambda t: (0, 0)),
            vmem,
            vmem,
        ],
        out_specs=[
            pl.BlockSpec((3, capacity, 8 * pair), lambda t: (0, 0, t)),
            pl.BlockSpec((8, 4, head_size), lambda t: (t, 0, 0)),
        ],
        out_shape=[
            jax.ShapeDtypeStruct((3, capacity, width), jnp.bfloat16),
            jax.ShapeDtypeStruct((bands, 4, head_size), jnp.float32),
        ],
        scratch_shapes=[
            pltpu.VMEM((3 * capacity, lines), jnp.bfloat16),
            pltpu.VMEM((capacity, lines), jnp.bfloat16),
            pltpu.VMEM((capacity, capacity), jnp.float32),
        ],
        compiler_params=pltpu.CompilerParams(vmem_limit_bytes=24 << 20),
        name="attend_pack",
    )
    gradients, gain_parts = attend(place, table, block_clip, arrived, chunks)
    by_head = lax.all_to_all(gain_parts, "seq", split_axis=0, concat_axis=0, tiled=True)
    mine = jnp.sum(by_head, axis=0, keepdims=True)
    every = lax.all_to_all(
        jnp.broadcast_to(mine, (loaders, 4, head_size)), ("chip", "core"), split_axis=0, concat_axis=0, tiled=True
    )
    gain_total = jnp.sum(every, axis=0).reshape(2, 2, head_size)
    return (gradients[:, None], gain_total)


def solution(mesh):
    chips, bands = mesh.devices.shape[0] // 2, mesh.devices.shape[1]
    mesh = jax.sharding.Mesh(mesh.devices.reshape(chips, 2, bands), ("chip", "core", "seq"))
    dp = ("chip", "core")
    in_specs = (P(None, dp, "seq", None), P(dp, None, "seq"), P(None, "seq", None), P(), P())
    out_specs = (P(None, dp, "seq", None), P(None, "seq", None))
    return jax.shard_map(shards, mesh=mesh, in_specs=in_specs, out_specs=out_specs, check_vma=False)
```

```python
import functools
import math

import jax
import jax.numpy as jnp
from jax import lax
from jax.experimental import pallas as pl
from jax.experimental.pallas import tpu as pltpu
from jax.sharding import PartitionSpec as P


epsilon = 1e-06
SLOTS = 3
EXTRA = 8
GROUP = 8


def iota(shape, axis):
    return lax.broadcasted_iota(jnp.int32, shape, axis)


def dot(left, right, left_axis=1, right_axis=0):
    return lax.dot_general(
        left,
        right,
        (((left_axis,), (right_axis,)), ((), ())),
        preferred_element_type=jnp.float32,
    )


def gather_kernel(
    flip, loaders, bands, capacity, place_ref, table_ref, rows_ref, out_ref, pick_ref, pick_last_ref, last_ref
):
    peers = loaders // 2
    lines = peers * GROUP
    half = 128 * last_ref.shape[0] // 2
    steps = rows_ref.shape[1] // (2 * half)
    me = place_ref[0]
    my_loader = me // bands
    column = iota((1, loaders * bands), 1)
    target = jnp.where(column % bands == me % bands, column // bands, -1)
    owner = 2 * iota((peers, 1), 0) + (my_loader + flip) % 2
    before = jnp.where((target < owner) & (target >= 0), 1.0, 0.0)
    same = jnp.where(target == owner, 1.0, 0.0)
    table = table_ref[...].astype(jnp.float32).astype(jnp.bfloat16)
    sums = dot(jnp.concatenate([before, same], axis=0).astype(jnp.bfloat16), table)
    sums = jnp.sum(jnp.where(iota(sums.shape, 1) == my_loader, sums, 0.0), axis=1, keepdims=True)
    start, count = sums[:peers].astype(jnp.int32), sums[peers:].astype(jnp.int32)
    last_column = jnp.where(count > SLOTS - 1, start + (SLOTS - 1), -1)
    pick_last_ref[...] = jnp.where(iota((peers, capacity), 1) == last_column, 1.0, 0.0).astype(jnp.bfloat16)
    spread = jnp.where(iota((lines, 1), 0) // GROUP == iota((1, peers), 1), 1.0, 0.0).astype(jnp.bfloat16)
    wide = dot(spread, jnp.concatenate([start, count], axis=1).astype(jnp.float32).astype(jnp.bfloat16))
    start, count = wide[:, 0:1].astype(jnp.int32), wide[:, 1:2].astype(jnp.int32)
    kind = iota((lines, 1), 0) % GROUP
    slot = kind // 3
    line_column = jnp.where(slot < count, (kind - 3 * slot) * capacity + start + slot, -1)
    lanes = iota((lines, 3 * capacity), 1)
    pick_ref[...] = jnp.where(lanes == line_column, 1.0, 0.0).astype(jnp.bfloat16)
    for step in range(steps):
        at = slice(2 * step * half, 2 * (step + 1) * half)
        out_ref[:, at] = dot(pick_ref[...], rows_ref[:, at]).astype(jnp.bfloat16)
        last = dot(pick_last_ref[...], rows_ref[2 * capacity :, at])
        for part in range(2):
            unit = 2 * step + part
            for low in range(0, half, 128):
                tile = (unit // GROUP) * (half // 128) + low // 128
                lane = part * half + low
                last_ref[tile, pl.ds(unit % GROUP, peers, stride=GROUP), :] = last[:, lane : lane + 128]
    for tile in range(last_ref.shape[0]):
        at = slice(rows_ref.shape[1] + tile * 128, rows_ref.shape[1] + (tile + 1) * 128)
        out_ref[:, at] = last_ref[tile].astype(jnp.bfloat16)


def chunk_kernel(capacity, cot_ref, gains_ref, out_ref):
    head_size = out_ref.shape[2]
    row = iota((EXTRA, head_size), 0)
    extra = jnp.zeros(row.shape, jnp.float32)
    for kind in range(2):
        for head in range(2):
            line = gains_ref[kind, head : head + 1, :]
            for part in range(2):
                piece = line.astype(jnp.bfloat16).astype(jnp.float32)
                extra = jnp.where(row == 4 * part + 2 * kind + head, piece, extra)
                line = line - piece
    extra = extra.astype(jnp.bfloat16)
    for chunk in range(cot_ref.shape[0]):
        for head in range(2):
            lanes = slice(head * head_size, (head + 1) * head_size)
            out_ref[chunk, head * capacity : (head + 1) * capacity] = cot_ref[chunk, :, lanes]
        out_ref[chunk, 2 * capacity :] = extra


def attention_kernel(
    loaders, bands, capacity, head_size,
    place_ref, table_ref, clip_ref, rows_ref, chunk_ref,
    grad_ref, gain_ref,
    pick_ref, pick_last_ref, same_ref,
):
    step = pl.program_id(0)
    lines = loaders * GROUP
    scale = 1.0 / math.sqrt(head_size)
    me = place_ref[0]
    my_core = (me // bands) % 2
    table_row = table_ref[pl.ds(me, 1), :]
    total = jnp.sum(table_row, axis=1, keepdims=True)
    valid = iota((capacity, 1), 0) < total

    @pl.when(step == 0)
    def _():
        counts = jnp.broadcast_to(table_row, (8, loaders)).astype(jnp.float32).astype(jnp.bfloat16)
        block = iota((loaders, lines), 1) // GROUP
        source = block - block % 2 + (block % 2 + my_core) % 2
        entry = iota((loaders, lines), 0)
        start = dot(counts, jnp.where(entry < source, 1.0, 0.0).astype(jnp.bfloat16))[:1].astype(jnp.int32)
        count = dot(counts, jnp.where(entry == source, 1.0, 0.0).astype(jnp.bfloat16))[:1].astype(jnp.int32)
        kind = iota((1, lines), 1) % GROUP
        slot = kind // 3
        place = iota((capacity, lines), 0)
        hit = (place == start + slot) & (slot < count)
        for part in range(3):
            pick_ref[part * capacity : (part + 1) * capacity] = jnp.where(
                hit & (kind % 3 == part), 1.0, 0.0
            ).astype(jnp.bfloat16)
        hit_last = (place == start + (SLOTS - 1)) & (count > SLOTS - 1)
        pick_last_ref[...] = jnp.where(hit_last, 1.0, 0.0).astype(jnp.bfloat16)
        clip_row = clip_ref[pl.ds(me // bands, 1), :]
        clip_lines = dot(
            jnp.broadcast_to(clip_row, (8, loaders)).astype(jnp.float32).astype(jnp.bfloat16),
            jnp.where(entry == source, 1.0, 0.0).astype(jnp.bfloat16),
        )[:1].astype(jnp.int32)
        first = kind == 0
        owned = (place >= start) & (place < start + count) & first
        owned = jnp.where(owned, 1.0, 0.0).astype(jnp.bfloat16)
        label_is = jnp.where(iota((16, lines), 0) == clip_lines, 1.0, 0.0).astype(jnp.bfloat16)
        label = dot(owned, label_is, 1, 1)
        label = jnp.where(iota((capacity, 16), 1) == 15, jnp.where(valid, 0.0, 1.0), label)
        label = label.astype(jnp.bfloat16)
        same_ref[...] = dot(label, label, 1, 1)

    same = same_ref[...] > 0.5
    group = iota((capacity, lines), 1) % GROUP
    width = 2 * head_size
    heads = [slice(head * head_size, (head + 1) * head_size) for head in range(2)]
    in_head = iota((width, width), 0) // head_size == iota((width, width), 1) // head_size
    averager = jnp.where(in_head, 1.0 / head_size, 0.0).astype(jnp.bfloat16)
    bfloat = jnp.bfloat16

    def average(rows):
        return dot(rows, averager)

    def lane_average(rows):
        means = [jnp.mean(rows[:, lanes], axis=1, keepdims=True) for lanes in heads]
        return jnp.concatenate([jnp.broadcast_to(m, (rows.shape[0], head_size)) for m in means], axis=1)

    units = gain_ref.shape[1]
    base = units * step
    features = chunk_ref.shape[0] * width
    here = pl.ds(pl.multiple_of(base * width, units * width), units * width)
    last_here = pl.ds(pl.multiple_of(features + base // GROUP * width, width), width)
    pick_last = [
        jnp.where(group == (base + unit) % GROUP, pick_last_ref[...], jnp.zeros((), bfloat))
        for unit in range(units)
    ]
    packed = dot(pick_ref[...], rows_ref[:, here])
    last = dot(jnp.concatenate(pick_last, axis=0), rows_ref[:, last_here])
    lane = [slice(unit * width, (unit + 1) * width) for unit in range(units)]
    span = [slice(unit * capacity, (unit + 1) * capacity) for unit in range(units)]
    value = [(packed[2 * capacity :, lane[u]] + last[span[u]]).astype(bfloat) for u in range(units)]
    extra = [chunk_ref[base + u, 2 * capacity :].astype(jnp.float32) for u in range(units)]
    extra = [rows[0:4] + rows[4:8] for rows in extra]
    gains = [
        jnp.concatenate(
            [jnp.concatenate([rows[2 * kind : 2 * kind + 1], rows[2 * kind + 1 : 2 * kind + 2]], axis=1) for kind in range(2)],
            axis=0,
        )
        for rows in extra
    ]
    dout = [
        jnp.where(valid, chunk_ref[base + u, head * capacity : (head + 1) * capacity], jnp.zeros((), bfloat))
        for u in range(units)
        for head in range(2)
    ]
    raw = jnp.concatenate(
        [packed[part * capacity : (part + 1) * capacity, lane[u]] for part in range(2) for u in range(units)], axis=0
    )
    centred = raw - average(raw.astype(bfloat))
    factor = lax.rsqrt(lane_average(centred * centred) + epsilon)
    hat = centred * factor
    hats = [[hat[(part * units + u) * capacity :][:capacity] for u in range(units)] for part in range(2)]
    qn = [(hats[0][u] * gains[u][0:1]).astype(bfloat) for u in range(units)]
    kn = [(hats[1][u] * gains[u][1:2]).astype(bfloat) for u in range(units)]
    each = [(u, lanes) for u in range(units) for lanes in heads]
    score = [dot(kn[u][:, lanes], qn[u][:, lanes], 1, 1) for u, lanes in each]
    dprob = [dot(value[u][:, lanes], dout[n], 1, 1) for n, (u, lanes) in enumerate(each)]
    weight = [jnp.where(same, jnp.exp(rows * scale), 0.0) for rows in score]
    prob = [rows * (1.0 / jnp.sum(rows, axis=0, keepdims=True)) for rows in weight]
    delta = [jnp.sum(p * d, axis=0, keepdims=True) for p, d in zip(prob, dprob)]
    dscore = [(p * (d - e)).astype(bfloat) for p, d, e in zip(prob, dprob, delta)]
    grads = [
        [dot(dscore[n], kn[u][:, lanes], 0, 0) for n, (u, lanes) in enumerate(each)],
        [dot(dscore[n], qn[u][:, lanes]) for n, (u, lanes) in enumerate(each)],
    ]
    dvalue = [dot(prob[n].astype(bfloat), dout[n]) for n in range(len(each))]
    for n, (u, lanes) in enumerate(each):
        grad_ref[2, :, u * width + lanes.start : u * width + lanes.stop] = dvalue[n].astype(bfloat)
    scaled, seconds = [], []
    for part in range(2):
        for u in range(units):
            grad = jnp.concatenate(grads[part][2 * u : 2 * u + 2], axis=1)
            gain = gains[u][part : part + 1] * scale
            product = grad * hats[part][u]
            total_gain = jnp.sum(product, axis=0, keepdims=True) * scale
            for head, lanes in enumerate(heads):
                for copy in range(2):
                    gain_ref[copy, u, 2 * part + head : 2 * part + head + 1, :] = total_gain[:, lanes]
            scaled.append(grad * gain)
            seconds.append(product * gain)
    scaled = jnp.concatenate(scaled, axis=0)
    first = lane_average(scaled)
    second = average(jnp.concatenate(seconds, axis=0).astype(bfloat))
    result = (factor * (scaled - first - hat * second)).astype(bfloat)
    for part in range(2):
        for u in range(units):
            grad_ref[part, :, lane[u]] = result[(part * units + u) * capacity :][:capacity]


def shards(loader_rows, cotangent, gains, block_rows, block_clip):
    loaders = lax.axis_size("chip") * 2
    bands = lax.axis_size("seq")
    capacity = loader_rows.shape[2]
    width = loader_rows.shape[3]
    head_size = gains.shape[2]
    lines = loaders * GROUP
    pair = 2 * head_size
    pairs = width // pair
    place = lax.axis_index(("chip", "core", "seq")).astype(jnp.int32).reshape(1)
    table = block_rows.reshape(loaders * bands, loaders)
    smem = pl.BlockSpec(memory_space=pltpu.SMEM)
    vmem = pl.BlockSpec(memory_space=pltpu.VMEM)

    vmem = pl.BlockSpec(memory_space=pltpu.VMEM)
    def gather(flip):
        return pl.pallas_call(
            functools.partial(gather_kernel, flip, loaders, bands, capacity),
            in_specs=[smem, vmem, vmem],
            out_specs=vmem,
            out_shape=jax.ShapeDtypeStruct((lines // 2, width + 2 * pair), jnp.bfloat16),
            scratch_shapes=[
                pltpu.VMEM((lines // 2, 3 * capacity), jnp.bfloat16),
                pltpu.VMEM((loaders // 2, capacity), jnp.bfloat16),
                pltpu.VMEM((2 * pair // 128, lines // 2, 128), jnp.float32),
            ],
            compiler_params=pltpu.CompilerParams(vmem_limit_bytes=8 << 20),
            cost_estimate=pl.CostEstimate(flops=300_000_000, bytes_accessed=3_000_000, transcendentals=0),
            name="gather_rows" if flip else "gather_own",
        )(place, table, loader_rows.reshape(3 * capacity, width))

    pack = pl.pallas_call(
        functools.partial(chunk_kernel, capacity),
        in_specs=[vmem, vmem],
        out_specs=vmem,
        out_shape=jax.ShapeDtypeStruct((bands, 2 * capacity + EXTRA, head_size), jnp.bfloat16),
        compiler_params=pltpu.CompilerParams(vmem_limit_bytes=8 << 20),
        name="chunk_cotangent",
    )
    chunks = pack(cotangent.reshape(bands, capacity, pair), gains)
    other = gather(1)
    other = lax.ppermute(other, "core", [(0, 1), (1, 0)])
    own = gather(0)
    shape = (loaders // 2, 1, GROUP, width + 2 * pair)
    outgoing = jnp.concatenate([own.reshape(shape), other.reshape(shape)], axis=1)

    def move_rows(rows):
        return lax.all_to_all(rows, "chip", split_axis=0, concat_axis=0, tiled=True)

    def move_chunks(chunks):
        return lax.all_to_all(chunks, "seq", split_axis=0, concat_axis=0, tiled=True)

    def rows_first(rows, chunks):
        rows, chunks = lax.optimization_barrier((move_rows(rows), chunks))
        return rows, move_chunks(chunks)

    def chunks_first(rows, chunks):
        rows, chunks = lax.optimization_barrier((rows, move_chunks(chunks)))
        return move_rows(rows), chunks

    arrived, chunks = lax.cond(lax.axis_index("core") == 0, rows_first, chunks_first, outgoing, chunks)
    arrived = arrived.reshape(lines, width + 2 * pair)

    attend = pl.pallas_call(
        functools.partial(attention_kernel, loaders, bands, capacity, head_size),
        grid=(pairs // 8,),
        in_specs=[
            smem,
            pl.BlockSpec((loaders * bands, loaders), lambda t: (0, 0)),
            pl.BlockSpec((loaders, loaders), lambda t: (0, 0)),
            vmem,
            vmem,
        ],
        out_specs=[
            pl.BlockSpec((3, capacity, 8 * pair), lambda t: (0, 0, t)),
            pl.BlockSpec((2, 8, 4, head_size), lambda t: (0, t, 0, 0)),
        ],
        out_shape=[
            jax.ShapeDtypeStruct((3, capacity, width), jnp.bfloat16),
            jax.ShapeDtypeStruct((2, bands, 4, head_size), jnp.float32),
        ],
        scratch_shapes=[
            pltpu.VMEM((3 * capacity, lines), jnp.bfloat16),
            pltpu.VMEM((capacity, lines), jnp.bfloat16),
            pltpu.VMEM((capacity, capacity), jnp.float32),
        ],
        compiler_params=pltpu.CompilerParams(vmem_limit_bytes=24 << 20),
        name="attend_pack",
    )
    gradients, gain_parts = attend(place, table, block_clip, arrived, chunks)
    by_head = lax.all_to_all(
        gain_parts.reshape(2 * bands, 4, head_size), ("core", "seq"), split_axis=0, concat_axis=0, tiled=True
    )
    mine = jnp.sum(by_head, axis=0, keepdims=True)
    every = lax.all_to_all(
        jnp.broadcast_to(mine, (loaders // 2, 4, head_size)), "chip", split_axis=0, concat_axis=0, tiled=True
    )
    gain_total = jnp.sum(every, axis=0).reshape(2, 2, head_size)
    return (gradients[:, None], gain_total)


def solution(mesh):
    chips, bands = mesh.devices.shape[0] // 2, mesh.devices.shape[1]
    mesh = jax.sharding.Mesh(mesh.devices.reshape(chips, 2, bands), ("chip", "core", "seq"))
    dp = ("chip", "core")
    in_specs = (P(None, dp, "seq", None), P(dp, None, "seq"), P(None, "seq", None), P(), P())
    out_specs = (P(None, dp, "seq", None), P(None, "seq", None))
    return jax.shard_map(shards, mesh=mesh, in_specs=in_specs, out_specs=out_specs, check_vma=False)
```
